256 devices in a mesh: energy: 16 (over z, core), block: 16 (over x, y).
Axes of the slice: x: 4, y: 4, z: 8, core: 2. Of those that a mesh axis runs over, the one named last changes fastest.
Arguments:
- g_lesser: float32 [2, 16, 4096, 256], P(None, 'energy', 'block'), may hold values from -0.75 to 0.75
- g_greater: float32 [2, 16, 4096, 256], P(None, 'energy', 'block'), may hold values from -0.75 to 0.75
- onsite: float32 [2, 16, 4096, 256], P(None, 'energy', 'block'), may hold values from -1 to 7
- lower: float32 [2, 4096, 256], P(None, 'block'), may hold values from -0.5 to 2.7
- upper: float32 [2, 4096, 256], P(None, 'block'), may hold values from -0.5 to 2.7
- rhs: float32 [2, 16, 4096, 128], P(None, 'energy', 'block'), may hold values from -16 to 16
Outputs:
- solution: float32 [2, 16, 4096, 128], P(None, 'energy', 'block')
The draws below stay inside these ranges and needn't reach their ends.
All inputs are finite; a program needn't handle non-finite values.
Results may differ from the reference program's by a relative error of at most 0.0003.
Values sent between devices are 32-bit elements; how exact they have to be, the bound alone decides.
No kernel may reach another device: no remote copies, remote signals or barrier semaphores. Data moves between devices by JAX's collectives and lax.ppermute only.
A program may use at most 64 MiB of HBM per device.

```python
import math
import jax
import jax.numpy as jnp
from jax import lax

BO = 256
NR = 128
NS_STEPS = 2
NE = 16
NB = 16
LEVELS = 4


def draw_onsite(key, part):
    first_key, second_key, third_key, fourth_key = jax.random.split(jax.random.fold_in(key, 11), 4)
    full_shape = (NE, NB * BO, BO)
    row_position = jnp.arange(NB * BO)[:, None] % BO
    column_position = jnp.arange(BO)[None, :]
    on_diagonal = (row_position == column_position).astype(jnp.float32)
    real_noise = jnp.clip(jax.random.normal(first_key, full_shape, jnp.float32), -4.0, 4.0)
    imag_noise = jnp.clip(jax.random.normal(second_key, full_shape, jnp.float32), -4.0, 4.0)
    real_diagonal = jax.random.uniform(third_key, full_shape, jnp.float32, 5.5, 6.5)
    imag_diagonal = jax.random.uniform(fourth_key, full_shape, jnp.float32, 0.2, 1.0)
    real_part = on_diagonal * real_diagonal + (1.0 - on_diagonal) * real_noise * (0.7 / math.sqrt(BO))
    imag_part = on_diagonal * imag_diagonal + (1.0 - on_diagonal) * imag_noise * (0.2 / math.sqrt(BO))
    return jnp.stack([real_part, imag_part])


def coupling_draw(key, draw_label):
    strength_key, real_key, imag_key = jax.random.split(jax.random.fold_in(key, draw_label), 3)
    full_shape = (NB * BO, BO)
    row_position = jnp.arange(NB * BO)[:, None] % BO
    column_position = jnp.arange(BO)[None, :]
    on_diagonal = (row_position == column_position).astype(jnp.float32)
    strength = jax.random.uniform(strength_key, full_shape, jnp.float32, 2.45, 2.7)
    real_noise = jnp.clip(jax.random.normal(real_key, full_shape, jnp.float32), -4.0, 4.0) * (0.7 / math.sqrt(BO))
    imag_noise = jnp.clip(jax.random.normal(imag_key, full_shape, jnp.float32), -4.0, 4.0) * (0.3 / math.sqrt(BO))
    real_part = on_diagonal * strength + (1.0 - on_diagonal) * real_noise
    return jnp.stack([real_part, imag_noise])


def draw_lower(key, part):
    return coupling_draw(key, 23)


def draw_upper(key, part):
    return coupling_draw(key, 37)


def block_scale(stream_key, dims, cuts, least, top_value):
    loudness, own = 1.0, jax.random.fold_in(stream_key, 6)
    for dim, shards_of in cuts:
        steps = jnp.exp(jax.random.uniform(jax.random.fold_in(own, dim), (shards_of,), jnp.float32, least / len(cuts), top_value / len(cuts)))
        loudness = loudness * jnp.repeat(steps, dims[dim] // shards_of).reshape([-1 if axis == dim else 1 for axis in range(len(dims))])
    return loudness


def bell_draw(rng, extent, deviation, reach, cuts=(), held_as=jnp.bfloat16):
    level = block_scale(rng, extent, cuts, -0.22, 0.18) if cuts else 1.0
    values = jax.random.normal(rng, extent, jnp.float32) * deviation * level
    return jnp.minimum(jnp.maximum(values, -reach), reach).astype(held_as)


def setup_inputs(seed: int = 0) -> dict:
    seeds = jax.random.split(jax.random.key(seed), 7)
    return {
        "g_lesser": bell_draw(seeds[0], (2, NE, NB * BO, BO), 0.12, 0.75, ((1, 16), (2, 16)), jnp.float32),
        "g_greater": bell_draw(seeds[1], (2, NE, NB * BO, BO), 0.12, 0.75, ((1, 16), (2, 16)), jnp.float32),
        "onsite": draw_onsite(jax.random.fold_in(seeds[6], 71), 0),
        "lower": draw_lower(jax.random.fold_in(seeds[6], 71), 0),
        "upper": draw_upper(jax.random.fold_in(seeds[6], 71), 0),
        "rhs": bell_draw(seeds[5], (2, NE, NB * BO, NR), 3.0, 16.0, ((1, 16), (2, 16)), jnp.float32),
    }


diagonal_guess = 5.0

def complex_product(left_factor, right_factor):
    exact_mode = lax.Precision.HIGHEST
    real_part = jnp.matmul(left_factor[0], right_factor[0], precision=exact_mode) - jnp.matmul(left_factor[1], right_factor[1], precision=exact_mode)
    imag_part = jnp.matmul(left_factor[0], right_factor[1], precision=exact_mode) + jnp.matmul(left_factor[1], right_factor[0], precision=exact_mode)
    return jnp.stack([real_part, imag_part])

def newton_inverse(matrix):
    block_order = matrix.shape[-1]
    identity = jnp.eye(block_order, dtype=jnp.float32)
    guess_real = jnp.broadcast_to(identity / diagonal_guess, matrix.shape[1:]).astype(jnp.float32)
    current = jnp.stack([guess_real, jnp.zeros_like(guess_real)])
    for sweep_index in range(NS_STEPS):
        product = complex_product(matrix, current)
        residue = jnp.stack([2.0 * identity - product[0], -product[1]])
        current = complex_product(current, residue)
    return current

def convolve(pair_arrays):
    lesser_part, greater_part = pair_arrays
    energies = lesser_part.shape[1]
    padded = jnp.concatenate([jnp.zeros_like(greater_part), greater_part], axis=1)

    def one_shift(offset):
        shifted = lax.dynamic_slice_in_dim(padded, (energies - offset).astype(jnp.int32), energies, 1)
        real_part = lax.optimization_barrier(jnp.sum(lesser_part[0] * shifted[0] - lesser_part[1] * shifted[1], axis=0))
        imag_part = lax.optimization_barrier(jnp.sum(lesser_part[0] * shifted[1] + lesser_part[1] * shifted[0], axis=0))
        return jnp.stack([real_part, imag_part])
    stacked = lax.map(one_shift, jnp.arange(energies, dtype=jnp.int32))
    return jnp.swapaxes(stacked, 0, 1) * (1.0 / math.sqrt(energies))

def from_before(values, stride):
    return jnp.concatenate([jnp.zeros_like(values[:, :, :stride]), values[:, :, :-stride]], axis=2)

def from_after(values, stride):
    return jnp.concatenate([values[:, :, stride:], jnp.zeros_like(values[:, :, :stride])], axis=2)

def reference(g_lesser, g_greater, onsite, lower, upper, rhs):
    lesser_blocks = g_lesser.reshape(2, NE, NB, BO, BO).transpose(2, 0, 1, 3, 4)
    greater_blocks = g_greater.reshape(2, NE, NB, BO, BO).transpose(2, 0, 1, 3, 4)
    polar = lax.map(convolve, (lesser_blocks, greater_blocks)).transpose(1, 2, 0, 3, 4)
    diag = onsite.reshape(2, NE, NB, BO, BO) - polar
    first_mask = (jnp.arange(NB) > 0).astype(jnp.float32)[None, :, None, None]
    last_mask = (jnp.arange(NB) < NB - 1).astype(jnp.float32)[None, :, None, None]
    lower_full = jnp.broadcast_to((lower.reshape(2, NB, BO, BO) * first_mask)[:, None], (2, NE, NB, BO, BO))
    upper_full = jnp.broadcast_to((upper.reshape(2, NB, BO, BO) * last_mask)[:, None], (2, NE, NB, BO, BO))
    source = rhs.reshape(2, NE, NB, BO, NR)
    for depth_index in range(LEVELS):
        stride = 1 << depth_index
        inverse = newton_inverse(diag)
        alpha = complex_product(inverse, lower_full)
        beta = complex_product(inverse, upper_full)
        rho = complex_product(inverse, source)
        alpha_left = from_before(alpha, stride)
        beta_left = from_before(beta, stride)
        rho_left = from_before(rho, stride)
        alpha_right = from_after(alpha, stride)
        beta_right = from_after(beta, stride)
        rho_right = from_after(rho, stride)
        diag = diag - complex_product(lower_full, beta_left) - complex_product(upper_full, alpha_right)
        source = source - complex_product(lower_full, rho_left) - complex_product(upper_full, rho_right)
        new_lower = -complex_product(lower_full, alpha_left)
        new_upper = -complex_product(upper_full, beta_right)
        lower_full = new_lower
        upper_full = new_upper
    solution = complex_product(newton_inverse(diag), source)
    return solution.reshape(2, NE, NB * BO, NR)
```

```python
import jax
import jax.numpy as jnp
from jax import lax
from jax.experimental import pallas as pl
from jax.experimental.pallas import tpu as pltpu
from jax.sharding import PartitionSpec as P


F32 = jnp.float32
BF16 = jnp.bfloat16
VMEM_LIMIT = 28 << 20
GUESS = 0.2


def split(value):
    high = value.astype(BF16)
    return high, (value - high.astype(F32)).astype(BF16)


def left_side(pair):
    sides = []
    for value in (pair[0], pair[1], pair[0] + pair[1]):
        high, low = split(value)
        sides.append(jnp.concatenate([high, high, low], axis=1))
    return sides


def real_product(side, value):
    high, low = split(value)
    return jnp.dot(
        side, jnp.concatenate([high, low, high], axis=0), preferred_element_type=F32
    )


def multiply(left, pair):
    real = real_product(left[0], pair[0])
    imag = real_product(left[1], pair[1])
    both = real_product(left[2], pair[0] + pair[1])
    return real - imag, both - real - imag


def load(ref):
    return ref[0], ref[1]


def save(ref, pair):
    ref[0] = pair[0]
    ref[1] = pair[1]


def minus(a, b):
    return a[0] - b[0], a[1] - b[1]


def negative(a):
    return -a[0], -a[1]


def choose(flag, a, b):
    return jnp.where(flag, a[0], b[0]), jnp.where(flag, a[1], b[1])


def columns_of(pair, start, stop):
    return pair[0][:, start:stop], pair[1][:, start:stop]


def newton_inverse(diag):
    order = diag[0].shape[0]
    rows = lax.broadcasted_iota(jnp.int32, (order, order), 0)
    columns = lax.broadcasted_iota(jnp.int32, (order, order), 1)
    identity = (rows == columns).astype(F32)
    base = (identity - diag[0] * GUESS, diag[1] * (-GUESS))
    left = left_side(base)
    square = multiply(left, base)
    cube = multiply(left, square)
    return (
        (identity + base[0] + square[0] + cube[0]) * GUESS,
        (base[1] + square[1] + cube[1]) * GUESS,
    )


def convolve_kernel(g_ref, out_ref):
    energies = g_ref.shape[0]
    scale = energies**-0.5

    def rows_of(step, carry):
        here = pl.ds(pl.multiple_of(step * 8, 8), 8)
        for offset in range(energies):
            real = imag = None
            for e in range(offset, energies):
                lr, li = g_ref[e, 0, here, :], g_ref[e, 1, here, :]
                gr, gi = g_ref[e - offset, 2, here, :], g_ref[e - offset, 3, here, :]
                re, im = lr * gr - li * gi, lr * gi + li * gr
                real = re if real is None else real + re
                imag = im if imag is None else imag + im
            out_ref[offset, 0, here, :] = real * scale
            out_ref[offset, 1, here, :] = imag * scale
        return carry

    lax.fori_loop(0, g_ref.shape[2] // 8, rows_of, 0)


def first_kernel(onsite_ref, polar_ref, diag_ref, inverse_ref):
    shape = onsite_ref.shape[1:]
    diag = tuple(onsite_ref[c] - polar_ref[:, c].reshape(shape) for c in range(2))
    save(diag_ref, diag)
    save(inverse_ref, newton_inverse(diag))


def level0_kernel(
    core_ref, diag_ref, lower_ref, upper_ref, xl_ref, xr_ref, hl_ref, ol_ref, hr_ref, or_ref,
    d_ref, l_ref, alpha_ref, inverse_ref, tl_ref, tr_ref,
):
    flag = core_ref[0] > 0
    diag = load(diag_ref)
    before = multiply(left_side(load(lower_ref)), load(xl_ref))
    save(tl_ref, before)
    left = left_side(before)
    zh, zo = multiply(left, load(hl_ref)), multiply(left, load(ol_ref))
    diag = minus(diag, choose(flag, zo, zh))
    new_lower = negative(choose(flag, zh, zo))
    save(l_ref, new_lower)
    after = multiply(left_side(load(upper_ref)), load(xr_ref))
    save(tr_ref, after)
    diag = minus(diag, multiply(left_side(after), choose(flag, load(hr_ref), load(or_ref))))
    save(d_ref, diag)
    inverse = newton_inverse(diag)
    save(inverse_ref, inverse)
    save(alpha_ref, multiply(left_side(inverse), new_lower))


def level0_rest_kernel(
    core_ref, rhs_ref, inverse_ref, tl_ref, tr_ref, hr_ref, or_ref, rl_ref, rr_ref,
    u_ref, r_ref, beta_ref, rho_ref,
):
    flag = core_ref[0] > 0
    source = minus(load(rhs_ref), multiply(left_side(load(tl_ref)), load(rl_ref)))
    after = left_side(load(tr_ref))
    new_upper = negative(multiply(after, choose(flag, load(or_ref), load(hr_ref))))
    source = minus(source, multiply(after, load(rr_ref)))
    save(u_ref, new_upper)
    save(r_ref, source)
    left = left_side(load(inverse_ref))
    save(beta_ref, multiply(left, new_upper))
    save(rho_ref, multiply(left, source))


def level1_first_kernel(
    flag_ref, diag_ref, lower_ref, upper_ref, rhs_ref, pa_ref, pb_ref, pr_ref,
    d_ref, p_ref, r_ref,
):
    flag = flag_ref[0] > 0
    left = left_side(choose(flag, load(upper_ref), load(lower_ref)))
    za, zb = multiply(left, load(pa_ref)), multiply(left, load(pb_ref))
    save(d_ref, minus(load(diag_ref), choose(flag, za, zb)))
    save(p_ref, negative(choose(flag, zb, za)))
    save(r_ref, minus(load(rhs_ref), multiply(left, load(pr_ref))))


def level1_kernel(
    flag_ref, diag_ref, lower_ref, upper_ref, rhs_ref, p_ref, qa_ref, qb_ref, qr_ref,
    d_ref, l_ref, u_ref, r_ref, coef_ref,
):
    flag = flag_ref[0] > 0
    n = diag_ref.shape[1]
    left = left_side(choose(flag, load(lower_ref), load(upper_ref)))
    za, zb = multiply(left, load(qa_ref)), multiply(left, load(qb_ref))
    diag = minus(load(diag_ref), choose(flag, zb, za))
    save(d_ref, diag)
    new_p, new_q = load(p_ref), negative(choose(flag, za, zb))
    source = minus(load(rhs_ref), multiply(left, load(qr_ref)))
    new_upper, new_lower = choose(flag, new_p, new_q), choose(flag, new_q, new_p)
    save(l_ref, new_lower)
    save(u_ref, new_upper)
    save(r_ref, source)
    left = left_side(newton_inverse(diag))
    for start, part in ((0, new_lower), (n, new_upper), (2 * n, source)):
        z = multiply(left, part)
        coef_ref[0, :, start : start + part[0].shape[1]] = z[0]
        coef_ref[1, :, start : start + part[0].shape[1]] = z[1]


def level2_kernel(
    flag_ref, diag_ref, lower_ref, upper_ref, rhs_ref, cl_ref, cr_ref,
    d_ref, r_ref, w_ref, coef_ref,
):
    flag = flag_ref[0] > 0
    n = diag_ref.shape[1]
    diag, source = load(diag_ref), load(rhs_ref)
    before, after = load(cl_ref), load(cr_ref)
    left_l, left_u = left_side(load(lower_ref)), left_side(load(upper_ref))
    z = multiply(left_l, columns_of(before, n, None))
    diag = minus(diag, columns_of(z, 0, n))
    source = minus(source, columns_of(z, n, None))
    diag = minus(diag, multiply(left_u, columns_of(after, 0, n)))
    source = minus(source, multiply(left_u, columns_of(after, 2 * n, None)))
    left = [jnp.where(flag, u, l) for u, l in zip(left_u, left_l)]
    other = choose(flag, columns_of(after, n, 2 * n), columns_of(before, 0, n))
    coupling = negative(multiply(left, other))
    save(d_ref, diag)
    save(r_ref, source)
    save(w_ref, coupling)
    left = left_side(newton_inverse(diag))
    for start, part in ((0, coupling), (n, source)):
        z = multiply(left, part)
        coef_ref[0, :, start : start + part[0].shape[1]] = z[0]
        coef_ref[1, :, start : start + part[0].shape[1]] = z[1]


def last_kernel(diag_ref, rhs_ref, w_ref, coef_ref, out_ref):
    n = diag_ref.shape[1]
    z = multiply(left_side(load(w_ref)), load(coef_ref))
    diag = minus(load(diag_ref), columns_of(z, 0, n))
    source = minus(load(rhs_ref), columns_of(z, n, None))
    save(out_ref, multiply(left_side(newton_inverse(diag)), source))


def run(kernel, out_shapes, args, products, scalars=0):
    outs = [jax.ShapeDtypeStruct(shape, F32) for shape in out_shapes]
    specs = [pl.BlockSpec(memory_space=pltpu.SMEM)] * scalars
    specs += [pl.BlockSpec(memory_space=pltpu.VMEM)] * (len(args) - scalars)
    moved = sum(a.size * 4 for a in args) + sum(o.size * 4 for o in outs)
    return pl.pallas_call(
        kernel,
        out_shape=outs,
        in_specs=specs,
        out_specs=[pl.BlockSpec(memory_space=pltpu.VMEM)] * len(outs),
        compiler_params=pltpu.CompilerParams(vmem_limit_bytes=VMEM_LIMIT),
        cost_estimate=pl.CostEstimate(
            flops=int(products * 24 * 256**3), bytes_accessed=moved, transcendentals=0
        ),
    )(*args)


def program(g_lesser, g_greater, onsite, lower, upper, rhs):
    energies, blocks = lax.axis_size("energy"), lax.axis_size("block")
    block = lax.axis_index("block")
    n, columns = onsite.shape[-1], rhs.shape[-1]
    share = n // energies
    onsite, rhs = onsite[:, 0], rhs[:, 0]

    def send(value, pairs):
        return lax.ppermute(value, "block", pairs)

    def shift(value, steps):
        return send(value, [(b, b + steps) for b in range(max(0, -steps), min(blocks, blocks - steps))])

    def flag(condition):
        return condition.astype(jnp.int32).reshape(1)

    first_core = lax.axis_index("energy") % 2 == 0
    half = jnp.where(
        first_core,
        jnp.where(block > 0, lower, 0.0),
        jnp.where(block < blocks - 1, upper, 0.0),
    )
    half_left, half_right = shift(half, 1), shift(half, -1)
    pairs = jnp.concatenate([g_lesser[:, 0], g_greater[:, 0]], axis=0)
    pairs = pairs.reshape(4, energies, share, n).swapaxes(0, 1)
    pairs = lax.all_to_all(pairs, "energy", split_axis=0, concat_axis=0, tiled=True)
    (polar,) = run(convolve_kernel, [(energies, 2, share, n)], [pairs], 0.02)
    core_flag, right_first, low_half = flag(first_core), flag(block & 2 == 0), flag(block < blocks // 2)
    polar, half_left, half_right, core_flag, right_first, low_half = lax.optimization_barrier(
        (polar, half_left, half_right, core_flag, right_first, low_half)
    )
    polar = lax.all_to_all(polar, "energy", split_axis=0, concat_axis=0, tiled=True)
    other = [(e, e ^ 1) for e in range(energies)]
    other_left = lax.ppermute(half_left, "energy", other)
    other_right = lax.ppermute(half_right, "energy", other)
    rhs_left, rhs_right = shift(rhs, 1), shift(rhs, -1)
    polar, other_left, other_right, rhs_left, rhs_right = lax.optimization_barrier(
        (polar, other_left, other_right, rhs_left, rhs_right)
    )

    square, wide = (2, n, n), (2, n, 2 * n + columns)
    slim, tall = (2, n, n + columns), (2, n, columns)
    diag, inverse = run(first_kernel, [square, square], [onsite, polar], 2)
    inverse_left, inverse_right = shift(inverse, 1), shift(inverse, -1)
    diag, low, alpha, inverse, through_left, through_right = run(
        level0_kernel,
        [square] * 6,
        [core_flag, diag, lower, upper, inverse_left, inverse_right, half_left, other_left, half_right, other_right],
        8,
        1,
    )
    up, source, beta, rho = run(
        level0_rest_kernel,
        [square, tall, square, tall],
        [core_flag, rhs, inverse, through_left, through_right, half_right, other_right, rhs_left, rhs_right],
        3.5,
        1,
    )

    across = [(b, b ^ 2) for b in range(blocks)]
    hand_on = [(b, b - 4 if b & 2 else b + 4) for b in range(blocks)]
    hand_on = [(b, t) for b, t in hand_on if 0 <= t < blocks]
    far = [(b, b + 2 if b & 2 else b - 2) for b in range(blocks)]
    far = [(b, t) for b, t in far if 0 <= t < blocks]

    swapped = [send(alpha, across), send(beta, across), send(rho, across)]
    handed = [send(swapped[0], hand_on), send(swapped[1], hand_on), send(rho, far)]
    diag, coupling, source = run(
        level1_first_kernel,
        [square, square, tall],
        [right_first, diag, low, up, source, *swapped],
        2.5,
        1,
    )
    diag, low, up, source, coef = run(
        level1_kernel,
        [square, square, square, tall, wide],
        [right_first, diag, low, up, source, coupling, *handed],
        7,
        1,
    )

    coef_left, coef_right = shift(coef, 4), shift(coef, -4)
    diag, source, coupling, coef = run(
        level2_kernel,
        [square, tall, square, slim],
        [low_half, diag, low, up, source, coef_left, coef_right],
        7.5,
        1,
    )
    coef = send(coef, [(b, b ^ 8) for b in range(blocks)])
    (solution,) = run(last_kernel, [tall], [diag, source, coupling, coef], 4)
    return solution[:, None]


def solution(mesh):
    placed = (
        P(None, "energy", "block", None),
        P(None, "energy", "block", None),
        P(None, "energy", "block", None),
        P(None, "block", None),
        P(None, "block", None),
        P(None, "energy", "block", None),
    )
    return jax.shard_map(
        program,
        mesh=mesh,
        in_specs=placed,
        out_specs=P(None, "energy", "block", None),
        check_vma=False,
    )
```

```python
import jax
import jax.numpy as jnp
from jax import lax
from jax.experimental import pallas as pl
from jax.experimental.pallas import tpu as pltpu
from jax.sharding import PartitionSpec as P


F32 = jnp.float32
BF16 = jnp.bfloat16
VMEM_LIMIT = 28 << 20
GUESS = 0.2


def split(value):
    high = value.astype(BF16)
    return high, (value - high.astype(F32)).astype(BF16)


def left_side(pair):
    sides = []
    for value in (pair[0], pair[1], pair[0] + pair[1]):
        high, low = split(value)
        sides.append(jnp.concatenate([high, high, low], axis=1))
    return sides


def real_product(side, value):
    high, low = split(value)
    return jnp.dot(
        side, jnp.concatenate([high, low, high], axis=0), preferred_element_type=F32
    )


def wide_product(left, pair):
    real = real_product(left[0], pair[0])
    imag = real_product(left[1], pair[1])
    both = real_product(left[2], pair[0] + pair[1])
    return real - imag, both - real - imag


def multiply(left, pair):
    columns = pair[0].shape[1]
    if columns > 128:
        return wide_product(left, pair)
    full = real_product(jnp.concatenate(left[:2], axis=0), jnp.concatenate(pair, axis=1))
    rows = left[0].shape[0]
    return (
        full[:rows, :columns] - full[rows:, columns:],
        full[:rows, columns:] + full[rows:, :columns],
    )


def load(ref):
    return ref[0], ref[1]


def save(ref, pair):
    ref[0] = pair[0]
    ref[1] = pair[1]


def minus(a, b):
    return a[0] - b[0], a[1] - b[1]


def negative(a):
    return -a[0], -a[1]


def choose(flag, a, b):
    return jnp.where(flag, a[0], b[0]), jnp.where(flag, a[1], b[1])


def columns_of(pair, start, stop):
    return pair[0][:, start:stop], pair[1][:, start:stop]


def step_matrix(diag):
    order = diag[0].shape[0]
    rows = lax.broadcasted_iota(jnp.int32, (order, order), 0)
    columns = lax.broadcasted_iota(jnp.int32, (order, order), 1)
    identity = (rows == columns).astype(F32)
    return identity, (identity - diag[0] * GUESS, diag[1] * (-GUESS))


def newton_inverse(diag):
    identity, base = step_matrix(diag)
    left = left_side(base)
    square = multiply(left, base)
    cube = multiply(left, square)
    return (
        (identity + base[0] + square[0] + cube[0]) * GUESS,
        (base[1] + square[1] + cube[1]) * GUESS,
    )


def newton_solve(diag, source):
    left = left_side(step_matrix(diag)[1])
    value = source
    for _ in range(3):
        z = wide_product(left, value)
        value = source[0] + z[0], source[1] + z[1]
    return value[0] * GUESS, value[1] * GUESS


def convolve_kernel(g_ref, out_ref):
    energies = g_ref.shape[0]
    scale = energies**-0.5
    here = pl.ds(pl.multiple_of(pl.program_id(0) * 8, 8), 8)
    for offset in range(energies):
        real = imag = None
        for e in range(offset, energies):
            lr, li = g_ref[e, 0, here, :], g_ref[e, 1, here, :]
            gr, gi = g_ref[e - offset, 2, here, :], g_ref[e - offset, 3, here, :]
            re, im = lr * gr - li * gi, lr * gi + li * gr
            real = re if real is None else real + re
            imag = im if imag is None else imag + im
        out_ref[offset, 0] = real * scale
        out_ref[offset, 1] = imag * scale


def convolve(pairs):
    energies, _, share, n = pairs.shape
    return pl.pallas_call(
        convolve_kernel,
        name="convolve",
        grid=(share // 8,),
        out_shape=jax.ShapeDtypeStruct((energies, 2, share, n), F32),
        in_specs=[pl.BlockSpec(memory_space=pltpu.VMEM)],
        out_specs=pl.BlockSpec((energies, 2, 8, n), lambda r: (0, 0, r, 0)),
        compiler_params=pltpu.CompilerParams(vmem_limit_bytes=VMEM_LIMIT),
        cost_estimate=pl.CostEstimate(
            flops=4 * energies**2 * share * n, bytes_accessed=6 * pairs.size, transcendentals=0
        ),
    )(pairs)


def first_kernel(onsite_ref, polar_ref, diag_ref, inverse_ref):
    shape = onsite_ref.shape[1:]
    diag = tuple(onsite_ref[c] - polar_ref[:, c].reshape(shape) for c in range(2))
    save(diag_ref, diag)
    save(inverse_ref, newton_inverse(diag))


def level0_kernel(
    core_ref, diag_ref, lower_ref, upper_ref, xl_ref, xr_ref, hl_ref, ol_ref, hr_ref, or_ref,
    d_ref, l_ref, alpha_ref, inverse_ref, tl_ref, tr_ref,
):
    flag = core_ref[0] > 0
    diag = load(diag_ref)
    before = multiply(left_side(load(lower_ref)), load(xl_ref))
    save(tl_ref, before)
    left = left_side(before)
    zh, zo = multiply(left, load(hl_ref)), multiply(left, load(ol_ref))
    diag = minus(diag, choose(flag, zo, zh))
    new_lower = negative(choose(flag, zh, zo))
    save(l_ref, new_lower)
    after = multiply(left_side(load(upper_ref)), load(xr_ref))
    save(tr_ref, after)
    diag = minus(diag, multiply(left_side(after), choose(flag, load(hr_ref), load(or_ref))))
    save(d_ref, diag)
    inverse = newton_inverse(diag)
    save(inverse_ref, inverse)
    save(alpha_ref, multiply(left_side(inverse), new_lower))


def level0_rest_kernel(
    core_ref, rhs_ref, inverse_ref, tl_ref, tr_ref, hr_ref, or_ref, rl_ref, rr_ref,
    u_ref, r_ref, beta_ref, rho_ref,
):
    flag = core_ref[0] > 0
    source = minus(load(rhs_ref), multiply(left_side(load(tl_ref)), load(rl_ref)))
    after = left_side(load(tr_ref))
    new_upper = negative(multiply(after, choose(flag, load(or_ref), load(hr_ref))))
    source = minus(source, multiply(after, load(rr_ref)))
    save(u_ref, new_upper)
    save(r_ref, source)
    left = left_side(load(inverse_ref))
    save(beta_ref, multiply(left, new_upper))
    save(rho_ref, multiply(left, source))


def level1_first_kernel(
    flag_ref, diag_ref, lower_ref, upper_ref, rhs_ref, pa_ref, pb_ref, pr_ref,
    d_ref, p_ref, r_ref,
):
    flag = flag_ref[0] > 0
    left = left_side(choose(flag, load(upper_ref), load(lower_ref)))
    za, zb = multiply(left, load(pa_ref)), multiply(left, load(pb_ref))
    save(d_ref, minus(load(diag_ref), choose(flag, za, zb)))
    save(p_ref, negative(choose(flag, zb, za)))
    save(r_ref, minus(load(rhs_ref), multiply(left, load(pr_ref))))


def level1_middle_kernel(
    flag_ref, diag_ref, lower_ref, upper_ref, rhs_ref, qa_ref, qr_ref, d_ref, q_ref, r_ref
):
    flag = flag_ref[0] > 0
    left = left_side(choose(flag, load(lower_ref), load(upper_ref)))
    za = multiply(left, load(qa_ref))
    diag = load(diag_ref)
    save(d_ref, choose(flag, diag, minus(diag, za)))
    save(q_ref, negative(za))
    save(r_ref, minus(load(rhs_ref), multiply(left, load(qr_ref))))


def level1_kernel(
    flag_ref, diag_ref, lower_ref, upper_ref, rhs_ref, p_ref, q_ref, qb_ref,
    d_ref, l_ref, u_ref, coef_ref,
):
    flag = flag_ref[0] > 0
    n = diag_ref.shape[1]
    left = left_side(choose(flag, load(lower_ref), load(upper_ref)))
    zb = multiply(left, load(qb_ref))
    diag = load(diag_ref)
    diag = choose(flag, minus(diag, zb), diag)
    save(d_ref, diag)
    new_p, new_q, source = load(p_ref), choose(flag, load(q_ref), negative(zb)), load(rhs_ref)
    new_upper, new_lower = choose(flag, new_p, new_q), choose(flag, new_q, new_p)
    save(l_ref, new_lower)
    save(u_ref, new_upper)
    left = left_side(newton_inverse(diag))
    for start, part in ((0, new_lower), (n, new_upper), (2 * n, source)):
        z = multiply(left, part)
        coef_ref[0, :, start : start + part[0].shape[1]] = z[0]
        coef_ref[1, :, start : start + part[0].shape[1]] = z[1]


def level2_kernel(
    flag_ref, diag_ref, lower_ref, upper_ref, rhs_ref, cl_ref, cr_ref,
    d_ref, r_ref, w_ref, coef_ref,
):
    flag = flag_ref[0] > 0
    n = diag_ref.shape[1]
    diag, source = load(diag_ref), load(rhs_ref)
    before, after = load(cl_ref), load(cr_ref)
    left_l, left_u = left_side(load(lower_ref)), left_side(load(upper_ref))
    diag = minus(diag, multiply(left_l, columns_of(before, n, 2 * n)))
    source = minus(source, multiply(left_l, columns_of(before, 2 * n, None)))
    diag = minus(diag, multiply(left_u, columns_of(after, 0, n)))
    source = minus(source, multiply(left_u, columns_of(after, 2 * n, None)))
    left = [jnp.where(flag, u, l) for u, l in zip(left_u, left_l)]
    other = choose(flag, columns_of(after, n, 2 * n), columns_of(before, 0, n))
    coupling = negative(multiply(left, other))
    save(d_ref, diag)
    save(r_ref, source)
    save(w_ref, coupling)
    left = left_side(newton_inverse(diag))
    for start, part in ((0, coupling), (n, source)):
        z = multiply(left, part)
        coef_ref[0, :, start : start + part[0].shape[1]] = z[0]
        coef_ref[1, :, start : start + part[0].shape[1]] = z[1]


def last_kernel(diag_ref, rhs_ref, w_ref, coef_ref, out_ref):
    n = diag_ref.shape[1]
    z = wide_product(left_side(load(w_ref)), load(coef_ref))
    source = minus(load(rhs_ref), columns_of(z, n, None))
    diag = minus(load(diag_ref), columns_of(z, 0, n))
    save(out_ref, newton_solve(diag, source))


def run(kernel, out_shapes, args, products, scalars=0):
    outs = [jax.ShapeDtypeStruct(shape, F32) for shape in out_shapes]
    specs = [pl.BlockSpec(memory_space=pltpu.SMEM)] * scalars
    specs += [pl.BlockSpec(memory_space=pltpu.VMEM)] * (len(args) - scalars)
    moved = sum(a.size * 4 for a in args) + sum(o.size * 4 for o in outs)
    return pl.pallas_call(
        kernel,
        out_shape=outs,
        in_specs=specs,
        out_specs=[pl.BlockSpec(memory_space=pltpu.VMEM)] * len(outs),
        compiler_params=pltpu.CompilerParams(vmem_limit_bytes=VMEM_LIMIT),
        cost_estimate=pl.CostEstimate(
            flops=int(products * 24 * 256**3), bytes_accessed=moved, transcendentals=0
        ),
    )(*args)


def program(g_lesser, g_greater, onsite, lower, upper, rhs):
    energies, blocks = lax.axis_size("energy"), lax.axis_size("block")
    block = lax.axis_index("block")
    n, columns = onsite.shape[-1], rhs.shape[-1]
    share = n // energies
    onsite, rhs = onsite[:, 0], rhs[:, 0]

    def send(value, pairs):
        return lax.ppermute(value, "block", pairs)

    def shift(value, steps):
        return send(value, [(b, b + steps) for b in range(max(0, -steps), min(blocks, blocks - steps))])

    def flag(condition):
        return condition.astype(jnp.int32).reshape(1)

    first_core = lax.axis_index("energy") % 2 == 0
    half = jnp.where(
        first_core,
        jnp.where(block > 0, lower, 0.0),
        jnp.where(block < blocks - 1, upper, 0.0),
    )
    half_left, half_right = shift(half, 1), shift(half, -1)
    pairs = jnp.concatenate([g_lesser[:, 0], g_greater[:, 0]], axis=0)
    pairs = pairs.reshape(4, energies, share, n).swapaxes(0, 1)
    pairs = lax.all_to_all(pairs, "energy", split_axis=0, concat_axis=0, tiled=True)
    polar = convolve(pairs)
    core_flag, right_first, low_half = flag(first_core), flag(block & 2 == 0), flag(block < blocks // 2)
    polar, half_left, half_right, core_flag, right_first, low_half = lax.optimization_barrier(
        (polar, half_left, half_right, core_flag, right_first, low_half)
    )
    polar = lax.all_to_all(polar, "energy", split_axis=0, concat_axis=0, tiled=True)
    other = [(e, e ^ 1) for e in range(energies)]
    other_left = lax.ppermute(half_left, "energy", other)
    other_right = lax.ppermute(half_right, "energy", other)
    rhs_left, rhs_right = shift(rhs, 1), shift(rhs, -1)
    polar, other_left, other_right, rhs_left, rhs_right = lax.optimization_barrier(
        (polar, other_left, other_right, rhs_left, rhs_right)
    )

    square, wide = (2, n, n), (2, n, 2 * n + columns)
    slim, tall = (2, n, n + columns), (2, n, columns)
    diag, inverse = run(first_kernel, [square, square], [onsite, polar], 2)
    inverse_left, inverse_right = shift(inverse, 1), shift(inverse, -1)
    diag, low, alpha, inverse, through_left, through_right = run(
        level0_kernel,
        [square] * 6,
        [core_flag, diag, lower, upper, inverse_left, inverse_right, half_left, other_left, half_right, other_right],
        8,
        1,
    )
    up, source, beta, rho = run(
        level0_rest_kernel,
        [square, tall, square, tall],
        [core_flag, rhs, inverse, through_left, through_right, half_right, other_right, rhs_left, rhs_right],
        3.5,
        1,
    )

    across = [(b, b ^ 2) for b in range(blocks)]
    hand_on = [(b, b - 4 if b & 2 else b + 4) for b in range(blocks)]
    hand_on = [(b, t) for b, t in hand_on if 0 <= t < blocks]
    far = [(b, b + 2 if b & 2 else b - 2) for b in range(blocks)]
    far = [(b, t) for b, t in far if 0 <= t < blocks]

    swapped = [send(alpha, across), send(beta, across), send(rho, across)]
    handed = [send(swapped[0], hand_on), send(swapped[1], hand_on), send(rho, far)]
    diag, coupling, source = run(
        level1_first_kernel,
        [square, square, tall],
        [right_first, diag, low, up, source, *swapped],
        2.5,
        1,
    )
    diag, mixed, source = run(
        level1_middle_kernel,
        [square, square, tall],
        [right_first, diag, low, up, source, handed[0], handed[2]],
        1.7,
        1,
    )
    diag, low, up, coef = run(
        level1_kernel,
        [square, square, square, wide],
        [right_first, diag, low, up, source, coupling, mixed, handed[1]],
        5.7,
        1,
    )

    coef_left, coef_right = shift(coef, 4), shift(coef, -4)
    diag, source, coupling, coef = run(
        level2_kernel,
        [square, tall, square, slim],
        [low_half, diag, low, up, source, coef_left, coef_right],
        7.5,
        1,
    )
    coef = send(coef, [(b, b ^ 8) for b in range(blocks)])
    (solution,) = run(last_kernel, [tall], [diag, source, coupling, coef], 4)
    return solution[:, None]


def solution(mesh):
    placed = (
        P(None, "energy", "block", None),
        P(None, "energy", "block", None),
        P(None, "energy", "block", None),
        P(None, "block", None),
        P(None, "block", None),
        P(None, "energy", "block", None),
    )
    return jax.shard_map(
        program,
        mesh=mesh,
        in_specs=placed,
        out_specs=P(None, "energy", "block", None),
        check_vma=False,
    )
```

```python
import jax
import jax.numpy as jnp
from jax import lax
from jax.experimental import pallas as pl
from jax.experimental.pallas import tpu as pltpu
from jax.sharding import PartitionSpec as P


F32 = jnp.float32
BF16 = jnp.bfloat16
VMEM_LIMIT = 28 << 20
GUESS = 0.2


def split(value):
    high = value.astype(BF16)
    return high, (value - high.astype(F32)).astype(BF16)


def left_side(pair):
    sides = []
    for value in (pair[0], pair[1], pair[0] + pair[1]):
        high, low = split(value)
        sides.append(jnp.concatenate([high, high, low], axis=1))
    return sides


def real_product(side, value):
    high, low = split(value)
    return jnp.dot(
        side, jnp.concatenate([high, low, high], axis=0), preferred_element_type=F32
    )


def wide_product(left, pair):
    real = real_product(left[0], pair[0])
    imag = real_product(left[1], pair[1])
    both = real_product(left[2], pair[0] + pair[1])
    return real - imag, both - real - imag


def multiply(left, pair):
    columns = pair[0].shape[1]
    if columns > 128:
        return wide_product(left, pair)
    full = real_product(jnp.concatenate(left[:2], axis=0), jnp.concatenate(pair, axis=1))
    rows = left[0].shape[0]
    return (
        full[:rows, :columns] - full[rows:, columns:],
        full[:rows, columns:] + full[rows:, :columns],
    )


def load(ref):
    return ref[0], ref[1]


def save(ref, pair):
    ref[0] = pair[0]
    ref[1] = pair[1]


def minus(a, b):
    return a[0] - b[0], a[1] - b[1]


def negative(a):
    return -a[0], -a[1]


def choose(flag, a, b):
    return jnp.where(flag, a[0], b[0]), jnp.where(flag, a[1], b[1])


def columns_of(pair, start, stop):
    return pair[0][:, start:stop], pair[1][:, start:stop]


def step_matrix(diag):
    order = diag[0].shape[0]
    rows = lax.broadcasted_iota(jnp.int32, (order, order), 0)
    columns = lax.broadcasted_iota(jnp.int32, (order, order), 1)
    identity = (rows == columns).astype(F32)
    return identity, (identity - diag[0] * GUESS, diag[1] * (-GUESS))


def newton_inverse(diag):
    identity, base = step_matrix(diag)
    left = left_side(base)
    square = multiply(left, base)
    cube = multiply(left, square)
    return (
        (identity + base[0] + square[0] + cube[0]) * GUESS,
        (base[1] + square[1] + cube[1]) * GUESS,
    )


def newton_solve(diag, source):
    left = left_side(step_matrix(diag)[1])
    value = source
    for _ in range(3):
        z = wide_product(left, value)
        value = source[0] + z[0], source[1] + z[1]
    return value[0] * GUESS, value[1] * GUESS


def convolve_kernel(g_ref, out_ref):
    energies = g_ref.shape[0]
    scale = energies**-0.5
    here = pl.ds(pl.multiple_of(pl.program_id(0) * 8, 8), 8)
    for offset in range(energies):
        real = imag = None
        for e in range(offset, energies):
            lr, li = g_ref[e, 0, here, :], g_ref[e, 1, here, :]
            gr, gi = g_ref[e - offset, 2, here, :], g_ref[e - offset, 3, here, :]
            re, im = lr * gr - li * gi, lr * gi + li * gr
            real = re if real is None else real + re
            imag = im if imag is None else imag + im
        out_ref[offset, 0] = real * scale
        out_ref[offset, 1] = imag * scale


def convolve(pairs):
    energies, _, share, n = pairs.shape
    return pl.pallas_call(
        convolve_kernel,
        name="convolve",
        grid=(share // 8,),
        out_shape=jax.ShapeDtypeStruct((energies, 2, share, n), F32),
        in_specs=[pl.BlockSpec(memory_space=pltpu.VMEM)],
        out_specs=pl.BlockSpec((energies, 2, 8, n), lambda r: (0, 0, r, 0)),
        compiler_params=pltpu.CompilerParams(vmem_limit_bytes=VMEM_LIMIT),
        cost_estimate=pl.CostEstimate(
            flops=4 * energies**2 * share * n, bytes_accessed=6 * pairs.size, transcendentals=0
        ),
    )(pairs)


def first_kernel(onsite_ref, polar_ref, diag_ref, inverse_ref):
    shape = onsite_ref.shape[1:]
    diag = tuple(onsite_ref[c] - polar_ref[:, c].reshape(shape) for c in range(2))
    save(diag_ref, diag)
    save(inverse_ref, newton_inverse(diag))


def level0_after_kernel(core_ref, diag_ref, upper_ref, xr_ref, hr_ref, or_ref, d_ref, tr_ref):
    flag = core_ref[0] > 0
    after = multiply(left_side(load(upper_ref)), load(xr_ref))
    save(tr_ref, after)
    z = multiply(left_side(after), choose(flag, load(hr_ref), load(or_ref)))
    save(d_ref, minus(load(diag_ref), z))


def level0_kernel(
    core_ref, diag_ref, lower_ref, xl_ref, hl_ref, ol_ref,
    d_ref, l_ref, alpha_ref, inverse_ref, tl_ref,
):
    flag = core_ref[0] > 0
    before = multiply(left_side(load(lower_ref)), load(xl_ref))
    save(tl_ref, before)
    left = left_side(before)
    zh, zo = multiply(left, load(hl_ref)), multiply(left, load(ol_ref))
    diag = minus(load(diag_ref), choose(flag, zo, zh))
    new_lower = negative(choose(flag, zh, zo))
    save(l_ref, new_lower)
    save(d_ref, diag)
    inverse = newton_inverse(diag)
    save(inverse_ref, inverse)
    save(alpha_ref, multiply(left_side(inverse), new_lower))


def level0_rest_kernel(
    core_ref, rhs_ref, inverse_ref, tl_ref, tr_ref, hr_ref, or_ref, rl_ref, rr_ref,
    u_ref, r_ref, beta_ref, rho_ref,
):
    flag = core_ref[0] > 0
    source = minus(load(rhs_ref), multiply(left_side(load(tl_ref)), load(rl_ref)))
    after = left_side(load(tr_ref))
    new_upper = negative(multiply(after, choose(flag, load(or_ref), load(hr_ref))))
    source = minus(source, multiply(after, load(rr_ref)))
    save(u_ref, new_upper)
    save(r_ref, source)
    left = left_side(load(inverse_ref))
    save(beta_ref, multiply(left, new_upper))
    save(rho_ref, multiply(left, source))


def level1_first_kernel(
    flag_ref, diag_ref, lower_ref, upper_ref, rhs_ref, pa_ref, pb_ref, pr_ref,
    d_ref, p_ref, r_ref,
):
    flag = flag_ref[0] > 0
    left = left_side(choose(flag, load(upper_ref), load(lower_ref)))
    za, zb = multiply(left, load(pa_ref)), multiply(left, load(pb_ref))
    save(d_ref, minus(load(diag_ref), choose(flag, za, zb)))
    save(p_ref, negative(choose(flag, zb, za)))
    save(r_ref, minus(load(rhs_ref), multiply(left, load(pr_ref))))


def level1_middle_kernel(
    flag_ref, diag_ref, lower_ref, upper_ref, rhs_ref, qa_ref, qr_ref, d_ref, q_ref, r_ref
):
    flag = flag_ref[0] > 0
    left = left_side(choose(flag, load(lower_ref), load(upper_ref)))
    za = multiply(left, load(qa_ref))
    diag = load(diag_ref)
    save(d_ref, choose(flag, diag, minus(diag, za)))
    save(q_ref, negative(za))
    save(r_ref, minus(load(rhs_ref), multiply(left, load(qr_ref))))


def level1_kernel(
    flag_ref, diag_ref, lower_ref, upper_ref, rhs_ref, p_ref, q_ref, qb_ref,
    d_ref, l_ref, u_ref, coef_ref,
):
    flag = flag_ref[0] > 0
    n = diag_ref.shape[1]
    left = left_side(choose(flag, load(lower_ref), load(upper_ref)))
    zb = multiply(left, load(qb_ref))
    diag = load(diag_ref)
    diag = choose(flag, minus(diag, zb), diag)
    save(d_ref, diag)
    new_p, new_q, source = load(p_ref), choose(flag, load(q_ref), negative(zb)), load(rhs_ref)
    new_upper, new_lower = choose(flag, new_p, new_q), choose(flag, new_q, new_p)
    save(l_ref, new_lower)
    save(u_ref, new_upper)
    left = left_side(newton_inverse(diag))
    for start, part in ((0, new_lower), (n, new_upper), (2 * n, source)):
        z = multiply(left, part)
        coef_ref[0, :, start : start + part[0].shape[1]] = z[0]
        coef_ref[1, :, start : start + part[0].shape[1]] = z[1]


def level2_after_kernel(diag_ref, upper_ref, rhs_ref, cr_ref, d_ref, r_ref, z_ref):
    n = diag_ref.shape[1]
    after, left = load(cr_ref), left_side(load(upper_ref))
    save(d_ref, minus(load(diag_ref), multiply(left, columns_of(after, 0, n))))
    save(r_ref, minus(load(rhs_ref), multiply(left, columns_of(after, 2 * n, None))))
    save(z_ref, multiply(left, columns_of(after, n, 2 * n)))


def level2_kernel(
    flag_ref, diag_ref, lower_ref, rhs_ref, z_ref, cl_ref,
    d_ref, r_ref, w_ref, coef_ref,
):
    flag = flag_ref[0] > 0
    n = diag_ref.shape[1]
    before, left = load(cl_ref), left_side(load(lower_ref))
    diag = minus(load(diag_ref), multiply(left, columns_of(before, n, 2 * n)))
    source = minus(load(rhs_ref), multiply(left, columns_of(before, 2 * n, None)))
    coupling = negative(choose(flag, load(z_ref), multiply(left, columns_of(before, 0, n))))
    save(d_ref, diag)
    save(r_ref, source)
    save(w_ref, coupling)
    left = left_side(newton_inverse(diag))
    for start, part in ((0, coupling), (n, source)):
        z = multiply(left, part)
        coef_ref[0, :, start : start + part[0].shape[1]] = z[0]
        coef_ref[1, :, start : start + part[0].shape[1]] = z[1]


def last_kernel(diag_ref, rhs_ref, w_ref, coef_ref, out_ref):
    n = diag_ref.shape[1]
    z = wide_product(left_side(load(w_ref)), load(coef_ref))
    source = minus(load(rhs_ref), columns_of(z, n, None))
    diag = minus(load(diag_ref), columns_of(z, 0, n))
    save(out_ref, newton_solve(diag, source))


def run(kernel, out_shapes, args, products, scalars=0):
    outs = [jax.ShapeDtypeStruct(shape, F32) for shape in out_shapes]
    specs = [pl.BlockSpec(memory_space=pltpu.SMEM)] * scalars
    specs += [pl.BlockSpec(memory_space=pltpu.VMEM)] * (len(args) - scalars)
    moved = sum(a.size * 4 for a in args) + sum(o.size * 4 for o in outs)
    return pl.pallas_call(
        kernel,
        out_shape=outs,
        in_specs=specs,
        out_specs=[pl.BlockSpec(memory_space=pltpu.VMEM)] * len(outs),
        compiler_params=pltpu.CompilerParams(vmem_limit_bytes=VMEM_LIMIT),
        cost_estimate=pl.CostEstimate(
            flops=int(products * 24 * 256**3), bytes_accessed=moved, transcendentals=0
        ),
    )(*args)


def program(g_lesser, g_greater, onsite, lower, upper, rhs):
    energies, blocks = lax.axis_size("energy"), lax.axis_size("block")
    block = lax.axis_index("block")
    n, columns = onsite.shape[-1], rhs.shape[-1]
    share = n // energies
    onsite, rhs = onsite[:, 0], rhs[:, 0]

    def send(value, pairs):
        return lax.ppermute(value, "block", pairs)

    def shift(value, steps):
        return send(value, [(b, b + steps) for b in range(max(0, -steps), min(blocks, blocks - steps))])

    def flag(condition):
        return condition.astype(jnp.int32).reshape(1)

    first_core = lax.axis_index("energy") % 2 == 0
    half = jnp.where(
        first_core,
        jnp.where(block > 0, lower, 0.0),
        jnp.where(block < blocks - 1, upper, 0.0),
    )
    half_left, half_right = shift(half, 1), shift(half, -1)
    pairs = jnp.concatenate([g_lesser[:, 0], g_greater[:, 0]], axis=0)
    pairs = pairs.reshape(4, energies, share, n).swapaxes(0, 1)
    pairs = lax.all_to_all(pairs, "energy", split_axis=0, concat_axis=0, tiled=True)
    polar = convolve(pairs)
    core_flag, right_first, low_half = flag(first_core), flag(block & 2 == 0), flag(block < blocks // 2)
    polar, half_left, half_right, core_flag, right_first, low_half = lax.optimization_barrier(
        (polar, half_left, half_right, core_flag, right_first, low_half)
    )
    polar = lax.all_to_all(polar, "energy", split_axis=0, concat_axis=0, tiled=True)
    other = [(e, e ^ 1) for e in range(energies)]
    other_left = lax.ppermute(half_left, "energy", other)
    other_right = lax.ppermute(half_right, "energy", other)
    rhs_left, rhs_right = shift(rhs, 1), shift(rhs, -1)
    polar, other_left, other_right, rhs_left, rhs_right = lax.optimization_barrier(
        (polar, other_left, other_right, rhs_left, rhs_right)
    )

    square, wide = (2, n, n), (2, n, 2 * n + columns)
    slim, tall = (2, n, n + columns), (2, n, columns)
    diag, inverse = run(first_kernel, [square, square], [onsite, polar], 2)
    inverse_right = shift(inverse, -1)
    inverse_left = shift(inverse, 1)
    diag, through_right = run(
        level0_after_kernel,
        [square] * 2,
        [core_flag, diag, upper, inverse_right, half_right, other_right],
        2,
        1,
    )
    diag, low, alpha, inverse, through_left = run(
        level0_kernel,
        [square] * 5,
        [core_flag, diag, lower, inverse_left, half_left, other_left],
        6,
        1,
    )
    up, source, beta, rho = run(
        level0_rest_kernel,
        [square, tall, square, tall],
        [core_flag, rhs, inverse, through_left, through_right, half_right, other_right, rhs_left, rhs_right],
        3.5,
        1,
    )

    across = [(b, b ^ 2) for b in range(blocks)]
    hand_on = [(b, b - 4 if b & 2 else b + 4) for b in range(blocks)]
    hand_on = [(b, t) for b, t in hand_on if 0 <= t < blocks]
    far = [(b, b + 2 if b & 2 else b - 2) for b in range(blocks)]
    far = [(b, t) for b, t in far if 0 <= t < blocks]

    swapped = [send(alpha, across), send(beta, across), send(rho, across)]
    handed = [send(swapped[0], hand_on), send(swapped[1], hand_on), send(rho, far)]
    diag, coupling, source = run(
        level1_first_kernel,
        [square, square, tall],
        [right_first, diag, low, up, source, *swapped],
        2.5,
        1,
    )
    diag, mixed, source = run(
        level1_middle_kernel,
        [square, square, tall],
        [right_first, diag, low, up, source, handed[0], handed[2]],
        1.7,
        1,
    )
    diag, low, up, coef = run(
        level1_kernel,
        [square, square, square, wide],
        [right_first, diag, low, up, source, coupling, mixed, handed[1]],
        5.7,
        1,
    )

    coef_right = shift(coef, -4)
    coef_left = shift(coef, 4)
    diag, source, mixed = run(
        level2_after_kernel, [square, tall, square], [diag, up, source, coef_right], 2.5
    )
    diag, source, coupling, coef = run(
        level2_kernel,
        [square, tall, square, slim],
        [low_half, diag, low, source, mixed, coef_left],
        6,
        1,
    )
    coef = send(coef, [(b, b ^ 8) for b in range(blocks)])
    (solution,) = run(last_kernel, [tall], [diag, source, coupling, coef], 4)
    return solution[:, None]


def solution(mesh):
    placed = (
        P(None, "energy", "block", None),
        P(None, "energy", "block", None),
        P(None, "energy", "block", None),
        P(None, "block", None),
        P(None, "block", None),
        P(None, "energy", "block", None),
    )
    return jax.shard_map(
        program,
        mesh=mesh,
        in_specs=placed,
        out_specs=P(None, "energy", "block", None),
        check_vma=False,
    )
```

```python
import jax
import jax.numpy as jnp
from jax import lax
from jax.experimental import pallas as pl
from jax.experimental.pallas import tpu as pltpu
from jax.sharding import PartitionSpec as P


F32 = jnp.float32
BF16 = jnp.bfloat16
VMEM_LIMIT = 28 << 20
GUESS = 0.2


def split(value):
    high = value.astype(BF16)
    return high, (value - high.astype(F32)).astype(BF16)


def left_side(pair):
    sides = []
    for value in (pair[0], pair[1], pair[0] + pair[1]):
        high, low = split(value)
        sides.append(jnp.concatenate([high, high, low], axis=1))
    return sides


def real_product(side, value):
    high, low = split(value)
    return jnp.dot(
        side, jnp.concatenate([high, low, high], axis=0), preferred_element_type=F32
    )


def wide_product(left, pair):
    real = real_product(left[0], pair[0])
    imag = real_product(left[1], pair[1])
    both = real_product(left[2], pair[0] + pair[1])
    return real - imag, both - real - imag


def multiply(left, pair):
    columns = pair[0].shape[1]
    if columns > 128:
        return wide_product(left, pair)
    full = real_product(jnp.concatenate(left[:2], axis=0), jnp.concatenate(pair, axis=1))
    rows = left[0].shape[0]
    return (
        full[:rows, :columns] - full[rows:, columns:],
        full[:rows, columns:] + full[rows:, :columns],
    )


def load(ref):
    return ref[0], ref[1]


def save(ref, pair):
    ref[0] = pair[0]
    ref[1] = pair[1]


def minus(a, b):
    return a[0] - b[0], a[1] - b[1]


def negative(a):
    return -a[0], -a[1]


def choose(flag, a, b):
    return jnp.where(flag, a[0], b[0]), jnp.where(flag, a[1], b[1])


def columns_of(pair, start, stop):
    return pair[0][:, start:stop], pair[1][:, start:stop]


def step_matrix(diag):
    order = diag[0].shape[0]
    rows = lax.broadcasted_iota(jnp.int32, (order, order), 0)
    columns = lax.broadcasted_iota(jnp.int32, (order, order), 1)
    identity = (rows == columns).astype(F32)
    return identity, (identity - diag[0] * GUESS, diag[1] * (-GUESS))


def newton_inverse(diag):
    identity, base = step_matrix(diag)
    left = left_side(base)
    square = multiply(left, base)
    cube = multiply(left, square)
    return (
        (identity + base[0] + square[0] + cube[0]) * GUESS,
        (base[1] + square[1] + cube[1]) * GUESS,
    )


def newton_solve(diag, source):
    left = left_side(step_matrix(diag)[1])
    value = source
    for _ in range(3):
        z = wide_product(left, value)
        value = source[0] + z[0], source[1] + z[1]
    return value[0] * GUESS, value[1] * GUESS


def convolve_kernel(g_ref, out_ref):
    energies = g_ref.shape[0]
    scale = energies**-0.5
    here = pl.ds(pl.multiple_of(pl.program_id(0) * 8, 8), 8)
    for offset in range(energies):
        real = imag = None
        for e in range(offset, energies):
            lr, li = g_ref[e, 0, here, :], g_ref[e, 1, here, :]
            gr, gi = g_ref[e - offset, 2, here, :], g_ref[e - offset, 3, here, :]
            re, im = lr * gr - li * gi, lr * gi + li * gr
            real = re if real is None else real + re
            imag = im if imag is None else imag + im
        out_ref[offset, 0] = real * scale
        out_ref[offset, 1] = imag * scale


def convolve(pairs):
    energies, _, share, n = pairs.shape
    return pl.pallas_call(
        convolve_kernel,
        name="convolve",
        grid=(share // 8,),
        out_shape=jax.ShapeDtypeStruct((energies, 2, share, n), F32),
        in_specs=[pl.BlockSpec(memory_space=pltpu.VMEM)],
        out_specs=pl.BlockSpec((energies, 2, 8, n), lambda r: (0, 0, r, 0)),
        compiler_params=pltpu.CompilerParams(vmem_limit_bytes=VMEM_LIMIT),
        cost_estimate=pl.CostEstimate(
            flops=4 * energies**2 * share * n, bytes_accessed=6 * pairs.size, transcendentals=0
        ),
    )(pairs)


def first_kernel(onsite_ref, polar_ref, diag_ref, inverse_ref):
    shape = onsite_ref.shape[1:]
    diag = tuple(onsite_ref[c] - polar_ref[:, c].reshape(shape) for c in range(2))
    save(diag_ref, diag)
    save(inverse_ref, newton_inverse(diag))


def level0_after_kernel(
    core_ref, diag_ref, upper_ref, xr_ref, hr_ref, or_ref, d_ref, u_ref, tr_ref
):
    flag = core_ref[0] > 0
    after = multiply(left_side(load(upper_ref)), load(xr_ref))
    save(tr_ref, after)
    left = left_side(after)
    zh, zo = multiply(left, load(hr_ref)), multiply(left, load(or_ref))
    save(d_ref, minus(load(diag_ref), choose(flag, zh, zo)))
    save(u_ref, negative(choose(flag, zo, zh)))


def level0_kernel(
    core_ref, diag_ref, lower_ref, upper_ref, xl_ref, hl_ref, ol_ref,
    d_ref, beta_ref, inverse_ref, tl_ref,
):
    flag = core_ref[0] > 0
    before = multiply(left_side(load(lower_ref)), load(xl_ref))
    save(tl_ref, before)
    z = multiply(left_side(before), choose(flag, load(ol_ref), load(hl_ref)))
    diag = minus(load(diag_ref), z)
    save(d_ref, diag)
    inverse = newton_inverse(diag)
    save(inverse_ref, inverse)
    save(beta_ref, multiply(left_side(inverse), load(upper_ref)))


def level0_rest_kernel(
    core_ref, rhs_ref, inverse_ref, tl_ref, tr_ref, hl_ref, ol_ref, rl_ref, rr_ref,
    l_ref, r_ref, alpha_ref, rho_ref,
):
    flag = core_ref[0] > 0
    before = left_side(load(tl_ref))
    new_lower = negative(multiply(before, choose(flag, load(hl_ref), load(ol_ref))))
    source = minus(load(rhs_ref), multiply(before, load(rl_ref)))
    source = minus(source, multiply(left_side(load(tr_ref)), load(rr_ref)))
    save(l_ref, new_lower)
    save(r_ref, source)
    left = left_side(load(inverse_ref))
    save(alpha_ref, multiply(left, new_lower))
    save(rho_ref, multiply(left, source))


def level1_first_kernel(
    flag_ref, diag_ref, lower_ref, upper_ref, rhs_ref, pa_ref, pb_ref, pr_ref,
    d_ref, p_ref, r_ref,
):
    flag = flag_ref[0] > 0
    left = left_side(choose(flag, load(upper_ref), load(lower_ref)))
    za, zb = multiply(left, load(pa_ref)), multiply(left, load(pb_ref))
    save(d_ref, minus(load(diag_ref), choose(flag, za, zb)))
    save(p_ref, negative(choose(flag, zb, za)))
    save(r_ref, minus(load(rhs_ref), multiply(left, load(pr_ref))))


def level1_middle_kernel(
    flag_ref, diag_ref, lower_ref, upper_ref, rhs_ref, qb_ref, qr_ref, d_ref, q_ref, r_ref
):
    flag = flag_ref[0] > 0
    left = left_side(choose(flag, load(lower_ref), load(upper_ref)))
    zb = multiply(left, load(qb_ref))
    diag = load(diag_ref)
    save(d_ref, choose(flag, minus(diag, zb), diag))
    save(q_ref, negative(zb))
    save(r_ref, minus(load(rhs_ref), multiply(left, load(qr_ref))))


def level1_kernel(
    flag_ref, diag_ref, lower_ref, upper_ref, rhs_ref, p_ref, q_ref, qa_ref,
    d_ref, l_ref, u_ref, coef_ref,
):
    flag = flag_ref[0] > 0
    n = diag_ref.shape[1]
    left = left_side(choose(flag, load(lower_ref), load(upper_ref)))
    za = multiply(left, load(qa_ref))
    diag = load(diag_ref)
    diag = choose(flag, diag, minus(diag, za))
    save(d_ref, diag)
    new_p, new_q, source = load(p_ref), choose(flag, negative(za), load(q_ref)), load(rhs_ref)
    new_upper, new_lower = choose(flag, new_p, new_q), choose(flag, new_q, new_p)
    save(l_ref, new_lower)
    save(u_ref, new_upper)
    left = left_side(newton_inverse(diag))
    for start, part in ((0, new_lower), (n, new_upper), (2 * n, source)):
        z = multiply(left, part)
        coef_ref[0, :, start : start + part[0].shape[1]] = z[0]
        coef_ref[1, :, start : start + part[0].shape[1]] = z[1]


def level2_after_kernel(diag_ref, upper_ref, rhs_ref, cr_ref, d_ref, r_ref, z_ref):
    n = diag_ref.shape[1]
    after, left = load(cr_ref), left_side(load(upper_ref))
    save(d_ref, minus(load(diag_ref), multiply(left, columns_of(after, 0, n))))
    save(r_ref, minus(load(rhs_ref), multiply(left, columns_of(after, 2 * n, None))))
    save(z_ref, multiply(left, columns_of(after, n, 2 * n)))


def level2_kernel(
    flag_ref, diag_ref, lower_ref, rhs_ref, z_ref, cl_ref,
    d_ref, r_ref, w_ref, coef_ref,
):
    flag = flag_ref[0] > 0
    n = diag_ref.shape[1]
    before, left = load(cl_ref), left_side(load(lower_ref))
    diag = minus(load(diag_ref), multiply(left, columns_of(before, n, 2 * n)))
    source = minus(load(rhs_ref), multiply(left, columns_of(before, 2 * n, None)))
    coupling = negative(choose(flag, load(z_ref), multiply(left, columns_of(before, 0, n))))
    save(d_ref, diag)
    save(r_ref, source)
    save(w_ref, coupling)
    left = left_side(newton_inverse(diag))
    for start, part in ((0, coupling), (n, source)):
        z = multiply(left, part)
        coef_ref[0, :, start : start + part[0].shape[1]] = z[0]
        coef_ref[1, :, start : start + part[0].shape[1]] = z[1]


def last_kernel(diag_ref, rhs_ref, w_ref, coef_ref, out_ref):
    n = diag_ref.shape[1]
    z = wide_product(left_side(load(w_ref)), load(coef_ref))
    source = minus(load(rhs_ref), columns_of(z, n, None))
    diag = minus(load(diag_ref), columns_of(z, 0, n))
    save(out_ref, newton_solve(diag, source))


def run(kernel, out_shapes, args, products, scalars=0):
    outs = [jax.ShapeDtypeStruct(shape, F32) for shape in out_shapes]
    specs = [pl.BlockSpec(memory_space=pltpu.SMEM)] * scalars
    specs += [pl.BlockSpec(memory_space=pltpu.VMEM)] * (len(args) - scalars)
    moved = sum(a.size * 4 for a in args) + sum(o.size * 4 for o in outs)
    return pl.pallas_call(
        kernel,
        out_shape=outs,
        in_specs=specs,
        out_specs=[pl.BlockSpec(memory_space=pltpu.VMEM)] * len(outs),
        compiler_params=pltpu.CompilerParams(vmem_limit_bytes=VMEM_LIMIT),
        cost_estimate=pl.CostEstimate(
            flops=int(products * 24 * 256**3), bytes_accessed=moved, transcendentals=0
        ),
    )(*args)


def program(g_lesser, g_greater, onsite, lower, upper, rhs):
    energies, blocks = lax.axis_size("energy"), lax.axis_size("block")
    block = lax.axis_index("block")
    n, columns = onsite.shape[-1], rhs.shape[-1]
    share = n // energies
    onsite, rhs = onsite[:, 0], rhs[:, 0]

    def send(value, pairs):
        return lax.ppermute(value, "block", pairs)

    def shift(value, steps):
        return send(value, [(b, b + steps) for b in range(max(0, -steps), min(blocks, blocks - steps))])

    def flag(condition):
        return condition.astype(jnp.int32).reshape(1)

    first_core = lax.axis_index("energy") % 2 == 0
    half = jnp.where(
        first_core,
        jnp.where(block > 0, lower, 0.0),
        jnp.where(block < blocks - 1, upper, 0.0),
    )
    half_left, half_right = shift(half, 1), shift(half, -1)
    pairs = jnp.concatenate([g_lesser[:, 0], g_greater[:, 0]], axis=0)
    pairs = pairs.reshape(4, energies, share, n).swapaxes(0, 1)
    pairs = lax.all_to_all(pairs, "energy", split_axis=0, concat_axis=0, tiled=True)
    polar = convolve(pairs)
    core_flag, right_first, low_half = flag(first_core), flag(block & 2 == 0), flag(block < blocks // 2)
    polar, half_left, half_right, core_flag, right_first, low_half = lax.optimization_barrier(
        (polar, half_left, half_right, core_flag, right_first, low_half)
    )
    polar = lax.all_to_all(polar, "energy", split_axis=0, concat_axis=0, tiled=True)
    other = [(e, e ^ 1) for e in range(energies)]
    other_left = lax.ppermute(half_left, "energy", other)
    other_right = lax.ppermute(half_right, "energy", other)
    rhs_left, rhs_right = shift(rhs, 1), shift(rhs, -1)
    polar, other_left, other_right, rhs_left, rhs_right = lax.optimization_barrier(
        (polar, other_left, other_right, rhs_left, rhs_right)
    )

    square, wide = (2, n, n), (2, n, 2 * n + columns)
    slim, tall = (2, n, n + columns), (2, n, columns)
    diag, inverse = run(first_kernel, [square, square], [onsite, polar], 2)
    inverse_right = shift(inverse, -1)
    inverse_left = shift(inverse, 1)
    diag, up, through_right = run(
        level0_after_kernel,
        [square] * 3,
        [core_flag, diag, upper, inverse_right, half_right, other_right],
        3,
        1,
    )
    diag, beta, inverse, through_left = run(
        level0_kernel,
        [square] * 4,
        [core_flag, diag, lower, up, inverse_left, half_left, other_left],
        5,
        1,
    )
    low, source, alpha, rho = run(
        level0_rest_kernel,
        [square, tall, square, tall],
        [core_flag, rhs, inverse, through_left, through_right, half_left, other_left, rhs_left, rhs_right],
        3.5,
        1,
    )

    across = [(b, b ^ 2) for b in range(blocks)]
    hand_on = [(b, b - 4 if b & 2 else b + 4) for b in range(blocks)]
    hand_on = [(b, t) for b, t in hand_on if 0 <= t < blocks]
    far = [(b, b + 2 if b & 2 else b - 2) for b in range(blocks)]
    far = [(b, t) for b, t in far if 0 <= t < blocks]

    swapped = [send(alpha, across), send(beta, across), send(rho, across)]
    handed = [send(swapped[0], hand_on), send(swapped[1], hand_on), send(rho, far)]
    diag, coupling, source = run(
        level1_first_kernel,
        [square, square, tall],
        [right_first, diag, low, up, source, *swapped],
        2.5,
        1,
    )
    diag, mixed, source = run(
        level1_middle_kernel,
        [square, square, tall],
        [right_first, diag, low, up, source, handed[1], handed[2]],
        1.7,
        1,
    )
    diag, low, up, coef = run(
        level1_kernel,
        [square, square, square, wide],
        [right_first, diag, low, up, source, coupling, mixed, handed[0]],
        5.7,
        1,
    )

    coef_right = shift(coef, -4)
    coef_left = shift(coef, 4)
    diag, source, mixed = run(
        level2_after_kernel, [square, tall, square], [diag, up, source, coef_right], 2.5
    )
    diag, source, coupling, coef = run(
        level2_kernel,
        [square, tall, square, slim],
        [low_half, diag, low, source, mixed, coef_left],
        6,
        1,
    )
    coef = send(coef, [(b, b ^ 8) for b in range(blocks)])
    (solution,) = run(last_kernel, [tall], [diag, source, coupling, coef], 4)
    return solution[:, None]


def solution(mesh):
    placed = (
        P(None, "energy", "block", None),
        P(None, "energy", "block", None),
        P(None, "energy", "block", None),
        P(None, "block", None),
        P(None, "block", None),
        P(None, "energy", "block", None),
    )
    return jax.shard_map(
        program,
        mesh=mesh,
        in_specs=placed,
        out_specs=P(None, "energy", "block", None),
        check_vma=False,
    )
```
